256 devices in a mesh: chan: 32 (over y_lo, z, core), tm: 8 (over y_hi, x).
Axes of the slice: x: 4, y: 4 (y_hi: 2, y_lo: 2; y = y_hi * 2 + y_lo), z: 8, core: 2. Of those that a mesh axis runs over, the one named last changes fastest.
Arguments:
- traces: bfloat16 [256, 6144], P('chan', 'tm'), may hold values from -6 to 6
- validity: int32 [256], P('chan'), may hold values 0 or 1
- owners: int32 [8], replicated, may hold values from 0 to 31
Outputs:
- correlations: float32 [8, 256, 8, 2048], P(None, 'chan', None, 'tm')
The draws below stay inside these ranges and needn't reach their ends.
All inputs are finite; a program needn't handle non-finite values. No bound on the sum of `validity` on one device may be relied on, other than what follows from the above.
Results may differ from the reference program's by a relative error of at most 0.0003.
Values may be sent and summed in bfloat16 or wider, within the bound.
No kernel may reach another device: no remote copies, remote signals or barrier semaphores. Data moves between devices by JAX's collectives and lax.ppermute only.
A program may use at most 64 MiB of HBM per device.

```python
import math
import jax
import jax.numpy as jnp
from jax import lax

CH_DEV = 8
TIME = 6144
LAG = 1024
STEPS = 8
CHANNELS = 256
N_CHAN = 32


def plant(array, rng, smallest, high):
    longest = array.shape.index(max(array.shape))
    spots = []
    for shift in (0, 1):
        where = [jax.random.randint(jax.random.fold_in(rng, axis), (), 0, length) for axis, length in enumerate(array.shape)]
        where[longest] = (where[longest] + shift) % array.shape[longest]
        spots.append(tuple(where))
    return array.at[spots[0]].set(smallest).at[spots[1]].set(high)


def shard_levels(key, dims, shards, smallest, high):
    def one(dim, blocks):
        steps = jax.random.uniform(jax.random.fold_in(jax.random.fold_in(key, 6), dim), (blocks,), jnp.float32, smallest / len(shards), high / len(shards))
        return jnp.repeat(jnp.exp(steps), dims[dim] // blocks).reshape((-1,) + (1,) * (len(dims) - dim - 1))

    loudness = one(*shards[0])
    for cut in shards[1:]:
        loudness = loudness * one(*cut)
    return loudness


def bell_draw(own_key, dims, width, reach, cuts=(), kind=jnp.bfloat16):
    array = jax.random.normal(own_key, dims, jnp.float32) * width
    if len(cuts) > 0:
        array = shard_levels(own_key, dims, cuts, -0.22, 0.18) * array
    return jnp.clip(array, min=-reach, max=reach).astype(kind)


def setup_inputs(seed: int = 0) -> dict:
    splits = jax.random.split(jax.random.key(seed), 4)
    traces = bell_draw(splits[0], (CHANNELS, TIME), 1.0, 6.0, ((0, 32), (1, 8)))
    validity = plant((jax.random.randint(splits[1], (CHANNELS,), 0, 8) < 7).astype(jnp.int32), jax.random.fold_in(splits[1], 1), 0, 1)
    owners = plant(jax.random.randint(splits[2], (STEPS,), 0, N_CHAN), jax.random.fold_in(splits[2], 1), 0, N_CHAN - 1).astype(jnp.int32)
    return dict(traces=traces, validity=validity, owners=owners)


def reference(traces, validity, owners):
    data = traces.astype(jnp.float32)
    fft_len = TIME + 2 * LAG
    spectra = jnp.fft.rfft(data, n=fft_len, axis=1)
    lag_index = (jnp.arange(2 * LAG) - LAG) % fft_len
    flags = validity.astype(jnp.float32)
    scale_factor = 1.0 / math.sqrt(TIME)

    def one_step(owner_index):
        begin_at = (owner_index * CH_DEV).astype(jnp.int32)
        source_spectra = lax.dynamic_slice_in_dim(spectra, begin_at, CH_DEV, 0)
        source_flags = lax.dynamic_slice_in_dim(flags, begin_at, CH_DEV, 0)
        cross_spectra = spectra[:, None, :] * jnp.conj(source_spectra)[None, :, :]
        circular = jnp.fft.irfft(cross_spectra, n=fft_len, axis=2)
        picked = circular[:, :, lag_index] * scale_factor
        return picked * flags[:, None, None] * source_flags[None, :, None]
    return lax.map(one_step, owners).astype(jnp.float32)
```

```python
import math

import jax
import jax.numpy as jnp
from jax import lax
from jax.experimental import pallas as pl
from jax.experimental.pallas import tpu as pltpu
from jax.sharding import Mesh, PartitionSpec as P

LAG = 1024
TIME = 6144
PIECE = 768
HALF = 384
FINE = 32
DEPTH = 6400
NAMES = ("y_lo", "z", "core", "y_hi", "x")
CHAN = ("y_lo", "z", "core")
TM = ("y_hi", "x")


def pick_kernel(owners_ref, row_ref, gathered_ref, out_ref):
    mine = row_ref[0]
    rows = [mine] + [owners_ref[s] for s in range(8)] + [mine + 1 - 2 * (mine % 2)]
    for place, row in enumerate(rows):
        block = gathered_ref[row]
        for peer in range(8):
            out_ref[peer, 8 * place : 8 * place + 8, :] = block


def pick(owners, row, gathered):
    return pl.pallas_call(
        pick_kernel,
        out_shape=jax.ShapeDtypeStruct((8, 80, HALF), jnp.bfloat16),
        in_specs=[pl.BlockSpec(memory_space=pltpu.SMEM)] * 2 + [pl.BlockSpec(memory_space=pltpu.VMEM)],
        out_specs=pl.BlockSpec(memory_space=pltpu.VMEM),
        compiler_params=pltpu.CompilerParams(vmem_limit_bytes=4 << 20),
    )(owners, row, gathered)


def corr_kernel(place_ref, own_ref, other_ref, out_ref, rec_ref, src_ref, h_ref):
    core = place_ref[0]
    m = place_ref[1]
    f32, bf16 = jnp.float32, jnp.bfloat16
    rec_ref[:, :LAG] = jnp.zeros((8, LAG), f32)
    rec_ref[:, LAG + TIME :] = jnp.zeros((8, rec_ref.shape[1] - LAG - TIME), f32)
    src_ref[:, :128] = jnp.zeros((256, 128), bf16)
    src_ref[:, 128 + TIME :] = jnp.zeros((256, src_ref.shape[1] - 128 - TIME), bf16)
    for piece in range(8):
        for ref, half, row in ((own_ref, core, 0), (other_ref, 1 - core, 72)):
            at = pl.multiple_of(PIECE * piece + HALF * half, 128)
            rec_ref[:, pl.ds(LAG + at, HALF)] = ref[piece, row : row + 8, :].astype(f32)
            src_ref[:64, pl.ds(128 + at, HALF)] = ref[piece, 8:72, :]
    lane = lax.broadcasted_iota(jnp.int32, (64, 128), 1)
    before = [None] * 4
    for k in range(src_ref.shape[1] // 128):
        tile = src_ref[:64, k * 128 : (k + 1) * 128].astype(f32)
        for i in range(1, 4):
            turned = pltpu.roll(tile, FINE * i, 1)
            if before[i] is not None:
                src_ref[64 * i : 64 * i + 64, k * 128 : (k + 1) * 128] = jnp.where(
                    lane < FINE * i, before[i], turned
                ).astype(bf16)
            before[i] = turned
    base = pl.multiple_of(256 * m, 128)
    lane32 = lax.broadcasted_iota(jnp.int32, (FINE, 128), 1)
    row32 = lax.broadcasted_iota(jnp.int32, (FINE, 128), 0)
    cross = lane32 + (FINE - 1) - row32 >= 128
    for r in range(8):
        last = None
        for k in range(DEPTH // 128 + 1):
            wide = jnp.broadcast_to(rec_ref[r : r + 1, pl.ds(base + k * 128, 128)], (FINE, 128))
            turned = pltpu.roll(wide, 128 - (FINE - 1), 1, stride=1, stride_axis=0)
            if last is not None:
                h_ref[FINE * r : FINE * r + FINE, (k - 1) * 128 : k * 128] = jnp.where(cross, turned, last).astype(bf16)
            last = turned
    scale = 1.0 / math.sqrt(TIME)
    spot = [FINE * rr + FINE - 1 - lane % FINE for rr in range(4)]
    for j in range(2):
        begin = 128 - 128 * j
        summed = lax.dot_general(
            src_ref[:, begin : begin + DEPTH], h_ref[...], (((1,), (1,)), ((), ())), preferred_element_type=f32
        )
        summed = summed * scale
        for q in range(2):
            parts = [summed[64 * i : 64 * i + 64, 128 * q : 128 * q + 128] for i in range(4)]
            for rr in range(4):
                row = None
                for i in range(4):
                    moved = jnp.take_along_axis(parts[i], spot[rr], axis=1)
                    row = moved if row is None else jnp.where(lane // FINE == i, moved, row)
                for s in range(8):
                    out_ref[s, 4 * q + rr, :, 128 * j : 128 * j + 128] = row[8 * s : 8 * s + 8]


def correlate(place, own, other):
    return pl.pallas_call(
        corr_kernel,
        out_shape=jax.ShapeDtypeStruct((8, 8, 8, 256), jnp.float32),
        in_specs=[pl.BlockSpec(memory_space=pltpu.SMEM)] + [pl.BlockSpec(memory_space=pltpu.VMEM)] * 2,
        out_specs=pl.BlockSpec(memory_space=pltpu.VMEM),
        scratch_shapes=[
            pltpu.VMEM((8, LAG + TIME + 1280), jnp.float32),
            pltpu.VMEM((256, 128 + DEPTH), jnp.bfloat16),
            pltpu.VMEM((256, DEPTH), jnp.bfloat16),
        ],
        compiler_params=pltpu.CompilerParams(vmem_limit_bytes=24 << 20),
    )(place, own, other)


def on_device(traces, validity, owners):
    usable = traces * validity.astype(jnp.bfloat16)[:, None]
    halves = usable.reshape(8, 2, HALF).transpose(1, 0, 2)
    gathered = lax.all_to_all(jnp.tile(halves, (16, 1, 1)), CHAN, 0, 0)
    row = lax.axis_index(CHAN)[None]
    sent = pick(owners, row, gathered)
    own = lax.all_to_all(sent, TM, 0, 0)
    other = lax.ppermute(own, "core", [(0, 1), (1, 0)])
    place = jnp.stack([lax.axis_index("core"), lax.axis_index(TM)])
    return correlate(place, own, other)


def solution(mesh):
    fine = Mesh(mesh.devices.reshape(2, 8, 2, 2, 4), NAMES)
    return jax.shard_map(
        on_device,
        mesh=fine,
        in_specs=(P(CHAN, TM), P(CHAN), P()),
        out_specs=P(None, CHAN, None, TM),
        check_vma=False,
    )
```

```python
import math

import jax
import jax.numpy as jnp
from jax import lax
from jax.experimental import pallas as pl
from jax.experimental.pallas import tpu as pltpu
from jax.sharding import Mesh, PartitionSpec as P

LAG = 1024
TIME = 6144
PIECE = 768
FINE = 32
DEPTH = 6400
NAMES = ("y_lo", "z", "core", "y_hi", "x")
CHAN = ("y_lo", "z", "core")
TM = ("y_hi", "x")
CHAN_ORDER = list(range(31, -1, -1))
TM_ORDER = list(range(7, -1, -1))
CHAN_GROUPS = [[8 * c + m for c in CHAN_ORDER] for m in range(8)]
TM_GROUPS = [[8 * c + m for m in TM_ORDER] for c in range(32)]
f32, bf16 = jnp.float32, jnp.bfloat16
VMEM = pl.BlockSpec(memory_space=pltpu.VMEM)
SMALL = pltpu.CompilerParams(vmem_limit_bytes=4 << 20)


def prepare_kernel(traces_hbm, validity_hbm, owners_hbm, blocks_ref, mine_ref, owners_ref, traces_ref, validity_ref, sems):
    moves = [
        pltpu.make_async_copy(src, dst, sems.at[n])
        for n, (src, dst) in enumerate(
            ((traces_hbm, traces_ref), (validity_hbm, validity_ref), (owners_hbm, owners_ref))
        )
    ]
    for move in moves:
        move.start()
    for move in moves:
        move.wait()
    row = lax.broadcasted_iota(jnp.int32, (8, 8), 0)
    lane = lax.broadcasted_iota(jnp.int32, (8, 8), 1)
    flags = jnp.broadcast_to(validity_ref[...].astype(f32), (8, 8))
    flags = jnp.sum(jnp.where(row == lane, flags, 0.0), axis=1, keepdims=True)
    usable = (traces_ref[...].astype(f32) * flags).astype(bf16)
    mine_ref[...] = usable
    for place, device in enumerate(CHAN_ORDER):
        half = device % 2
        blocks_ref[place] = usable[4 * half : 4 * half + 4]


def prepare(traces, validity, owners):
    inputs = [pltpu.with_memory_space_constraint(v, pltpu.HBM) for v in (traces, validity.reshape(1, 8), owners.reshape(1, 8))]
    return pl.pallas_call(
        prepare_kernel,
        out_shape=(
            jax.ShapeDtypeStruct((32, 4, PIECE), bf16),
            jax.ShapeDtypeStruct((8, PIECE), bf16),
            jax.ShapeDtypeStruct((1, 8), jnp.int32),
        ),
        in_specs=[pl.BlockSpec(memory_space=pltpu.HBM)] * 3,
        out_specs=(VMEM, VMEM, VMEM),
        scratch_shapes=[pltpu.VMEM((8, PIECE), bf16), pltpu.VMEM((1, 8), jnp.int32), pltpu.SemaphoreType.DMA((3,))],
        compiler_params=SMALL,
    )(*inputs)


def pick_kernel(owners_ref, mine_ref, gathered_ref, out_ref):
    lane = lax.broadcasted_iota(jnp.int32, (1, 8), 1)
    owners = owners_ref[...]
    for peer in range(8):
        out_ref[peer, :8, :] = mine_ref[...]
    for s in range(8):
        block = gathered_ref[31 - jnp.sum(jnp.where(lane == s, owners, 0))]
        for peer in range(8):
            out_ref[peer, 8 + 4 * s : 12 + 4 * s, :] = block


def pick(owners, mine, gathered):
    return pl.pallas_call(
        pick_kernel,
        out_shape=jax.ShapeDtypeStruct((8, 40, PIECE), bf16),
        in_specs=[VMEM] * 3,
        out_specs=VMEM,
        compiler_params=SMALL,
    )(owners, mine, gathered)


def load_sources(pieces_ref, src_ref):
    src_ref[:, :256] = jnp.zeros((256, 256), bf16)
    src_ref[:, 128 + TIME :] = jnp.zeros((256, DEPTH - TIME), bf16)
    lane = lax.broadcasted_iota(jnp.int32, (32, 128), 1)
    before = [None] * 4
    for k in range(1, DEPTH // 128 + 1):
        t = 128 * (k - 1)
        if t < TIME:
            tile = pieces_ref[7 - t // PIECE, 8:40, t % PIECE : t % PIECE + 128]
        else:
            tile = jnp.zeros((32, 128), bf16)
        wide = tile.astype(f32)
        for i in range(4):
            if i == 0:
                value = tile
            else:
                turned = pltpu.roll(wide, FINE * i, 1)
                last = before[i] if before[i] is not None else jnp.zeros((32, 128), f32)
                value = jnp.where(lane < FINE * i, last, turned).astype(bf16)
                before[i] = turned
            src_ref[32 * i : 32 * i + 32, 128 * k : 128 * k + 128] = value
            if k < DEPTH // 128:
                src_ref[128 + 32 * i : 160 + 32 * i, 128 * k + 128 : 128 * k + 256] = value


def spread_receivers(pieces_ref, rec_ref, h_ref):
    rec_ref[:, :LAG] = jnp.zeros((8, LAG), f32)
    rec_ref[:, LAG + TIME :] = jnp.zeros((8, rec_ref.shape[1] - LAG - TIME), f32)
    for piece in range(8):
        at = LAG + PIECE * piece
        rec_ref[:, at : at + PIECE] = pieces_ref[7 - piece, :8, :].astype(f32)
    base = pl.multiple_of(256 * lax.axis_index(TM), 128)
    lane = lax.broadcasted_iota(jnp.int32, (FINE, 128), 1)
    row = lax.broadcasted_iota(jnp.int32, (FINE, 128), 0)
    cross = lane + (FINE - 1) - row >= 128
    for r in range(8):
        last = None
        for k in range(DEPTH // 128 + 1):
            wide = jnp.broadcast_to(rec_ref[r : r + 1, pl.ds(base + k * 128, 128)], (FINE, 128))
            turned = pltpu.roll(wide, 128 - (FINE - 1), 1, stride=1, stride_axis=0)
            if last is not None:
                h_ref[FINE * r : FINE * r + FINE, (k - 1) * 128 : k * 128] = jnp.where(cross, turned, last).astype(bf16)
            last = turned


def correlate(src_ref, h_ref, emit):
    summed = lax.dot_general(
        src_ref[:, 128 : 128 + DEPTH], h_ref[...], (((1,), (1,)), ((), ())), preferred_element_type=f32
    )
    summed = summed * (1.0 / math.sqrt(TIME))
    lane = lax.broadcasted_iota(jnp.int32, (32, 128), 1)
    spot = [FINE * q + FINE - 1 - lane % FINE for q in range(4)]
    for j in range(2):
        for half in range(2):
            for q in range(4):
                rows = None
                for i in range(4):
                    at = 128 * j + 32 * i
                    moved = jnp.take_along_axis(summed[at : at + 32, 128 * half : 128 * half + 128], spot[q], axis=1)
                    rows = moved if rows is None else jnp.where(lane // FINE == i, moved, rows)
                emit(j, 4 * half + q, rows)


def first_kernel(pieces_ref, h_ref, part_ref, rec_ref, src_ref):
    load_sources(pieces_ref, src_ref)
    spread_receivers(pieces_ref, rec_ref, h_ref)

    def emit(j, r, rows):
        part_ref[r, j] = rows

    correlate(src_ref, h_ref, emit)


def second_kernel(pieces_ref, h_ref, part_ref, out_ref, src_ref):
    load_sources(pieces_ref, src_ref)
    first = lax.axis_index("core") == 0
    low = lax.broadcasted_iota(jnp.int32, (8, 128), 0) < 4

    def emit(j, r, rows):
        mine = part_ref[r, j]
        for a in range(4):
            x, y = mine[8 * a : 8 * a + 8], rows[8 * a : 8 * a + 8]
            x, y = jnp.where(first, x, y), jnp.where(first, y, x)
            lags = slice(128 * j, 128 * j + 128)
            out_ref[2 * a, r, :, lags] = jnp.where(low, x, pltpu.roll(y, 4, 0))
            out_ref[2 * a + 1, r, :, lags] = jnp.where(low, pltpu.roll(x, 4, 0), y)

    correlate(src_ref, h_ref, emit)


COST = pl.CostEstimate(flops=2 * 256 * 256 * DEPTH, bytes_accessed=4 << 20, transcendentals=0)
LARGE = pltpu.CompilerParams(vmem_limit_bytes=16 << 20)
SOURCES = pltpu.VMEM((256, 128 + DEPTH), bf16)


def on_device(traces, validity, owners):
    blocks, mine, owners = prepare(traces, validity, owners)
    gathered = lax.all_to_all(blocks, NAMES, 0, 0, axis_index_groups=CHAN_GROUPS)
    own = lax.all_to_all(pick(owners, mine, gathered), NAMES, 0, 0, axis_index_groups=TM_GROUPS)
    other = lax.ppermute(own, "core", [(0, 1), (1, 0)])
    spread, part = pl.pallas_call(
        first_kernel,
        out_shape=(jax.ShapeDtypeStruct((256, DEPTH), bf16), jax.ShapeDtypeStruct((8, 2, 32, 128), f32)),
        in_specs=[VMEM],
        out_specs=(VMEM, VMEM),
        scratch_shapes=[pltpu.VMEM((8, LAG + TIME + 1280), f32), SOURCES],
        compiler_params=LARGE,
        cost_estimate=COST,
    )(own)
    return pl.pallas_call(
        second_kernel,
        out_shape=jax.ShapeDtypeStruct((8, 8, 8, 256), f32),
        in_specs=[VMEM] * 3,
        out_specs=VMEM,
        scratch_shapes=[SOURCES],
        compiler_params=LARGE,
        cost_estimate=COST,
    )(other, spread, part)


def solution(mesh):
    fine = Mesh(mesh.devices.reshape(2, 8, 2, 2, 4), NAMES)
    return jax.shard_map(
        on_device,
        mesh=fine,
        in_specs=(P(CHAN, TM), P(CHAN), P()),
        out_specs=P(None, CHAN, None, TM),
        check_vma=False,
    )
```

```python
import math

import jax
import jax.numpy as jnp
from jax import lax
from jax.experimental import pallas as pl
from jax.experimental.pallas import tpu as pltpu
from jax.sharding import Mesh, PartitionSpec as P

LAG = 1024
TIME = 6144
PIECE = 768
FINE = 32
DEPTH = 6400
NAMES = ("y_lo", "z", "core", "y_hi", "x")
CHAN = ("y_lo", "z", "core")
TM = ("y_hi", "x")
CM, TMK = 27, 6
CHAN_ORDER = [k ^ CM for k in range(32)]
TM_ORDER = [k ^ TMK for k in range(8)]
CHAN_GROUPS = [[8 * c + m for c in CHAN_ORDER] for m in range(8)]
TM_GROUPS = [[8 * c + m for m in TM_ORDER] for c in range(32)]
f32, bf16 = jnp.float32, jnp.bfloat16
VMEM = pl.BlockSpec(memory_space=pltpu.VMEM)
SMALL = pltpu.CompilerParams(vmem_limit_bytes=4 << 20)


def prepare_kernel(traces_hbm, validity_hbm, owners_hbm, blocks_ref, mine_ref, owners_ref, traces_ref, validity_ref, sems):
    moves = [
        pltpu.make_async_copy(src, dst, sems.at[n])
        for n, (src, dst) in enumerate(
            ((traces_hbm, traces_ref), (validity_hbm, validity_ref), (owners_hbm, owners_ref))
        )
    ]
    for move in moves:
        move.start()
    for move in moves:
        move.wait()
    row = lax.broadcasted_iota(jnp.int32, (8, 8), 0)
    lane = lax.broadcasted_iota(jnp.int32, (8, 8), 1)
    flags = jnp.broadcast_to(validity_ref[...].astype(f32), (8, 8))
    flags = jnp.sum(jnp.where(row == lane, flags, 0.0), axis=1, keepdims=True)
    usable = (traces_ref[...].astype(f32) * flags).astype(bf16)
    mine_ref[...] = usable
    for place, device in enumerate(CHAN_ORDER):
        half = device % 2
        blocks_ref[place] = usable[4 * half : 4 * half + 4]


def prepare(traces, validity, owners):
    inputs = [pltpu.with_memory_space_constraint(v, pltpu.HBM) for v in (traces, validity.reshape(1, 8), owners.reshape(1, 8))]
    return pl.pallas_call(
        prepare_kernel,
        out_shape=(
            jax.ShapeDtypeStruct((32, 4, PIECE), bf16),
            jax.ShapeDtypeStruct((8, PIECE), bf16),
            jax.ShapeDtypeStruct((1, 8), jnp.int32),
        ),
        in_specs=[pl.BlockSpec(memory_space=pltpu.HBM)] * 3,
        out_specs=(VMEM, VMEM, VMEM),
        scratch_shapes=[pltpu.VMEM((8, PIECE), bf16), pltpu.VMEM((1, 8), jnp.int32), pltpu.SemaphoreType.DMA((3,))],
        compiler_params=SMALL,
    )(*inputs)


def pick_kernel(owners_ref, mine_ref, gathered_ref, out_ref):
    lane = lax.broadcasted_iota(jnp.int32, (1, 8), 1)
    owners = owners_ref[...]
    for peer in range(8):
        out_ref[peer, :8, :] = mine_ref[...]
    for s in range(8):
        block = gathered_ref[jnp.bitwise_xor(jnp.sum(jnp.where(lane == s, owners, 0)), CM)]
        for peer in range(8):
            out_ref[peer, 8 + 4 * s : 12 + 4 * s, :] = block


def pick(owners, mine, gathered):
    return pl.pallas_call(
        pick_kernel,
        out_shape=jax.ShapeDtypeStruct((8, 40, PIECE), bf16),
        in_specs=[VMEM] * 3,
        out_specs=VMEM,
        compiler_params=SMALL,
    )(owners, mine, gathered)


def start_sources(src_ref):
    src_ref[:, :256] = jnp.zeros((256, 256), bf16)


def load_sources(pieces_ref, src_ref, begin, end, before):
    lane = lax.broadcasted_iota(jnp.int32, (32, 128), 1)
    for k in range(begin, end):
        t = 128 * k
        if t < TIME:
            tile = pieces_ref[(t // PIECE) ^ TMK, 8:40, t % PIECE : t % PIECE + 128]
        else:
            tile = jnp.zeros((32, 128), bf16)
        wide = tile.astype(f32)
        for i in range(4):
            if i == 0:
                value = tile
            else:
                turned = pltpu.roll(wide, FINE * i, 1)
                last = before[i] if before[i] is not None else jnp.zeros((32, 128), f32)
                value = jnp.where(lane < FINE * i, last, turned).astype(bf16)
                before[i] = turned
            src_ref[32 * i : 32 * i + 32, 128 * k + 128 : 128 * k + 256] = value
            if k + 1 < DEPTH // 128:
                src_ref[128 + 32 * i : 160 + 32 * i, 128 * k + 256 : 128 * k + 384] = value


def start_receivers(pieces_ref, rec_ref):
    rec_ref[:, :LAG] = jnp.zeros((8, LAG), f32)
    rec_ref[:, LAG + TIME :] = jnp.zeros((8, rec_ref.shape[1] - LAG - TIME), f32)
    for piece in range(8):
        at = LAG + PIECE * piece
        rec_ref[:, at : at + PIECE] = pieces_ref[piece ^ TMK, :8, :].astype(f32)


def spread_receivers(rec_ref, h_ref, begin, end, before):
    base = pl.multiple_of(256 * lax.axis_index(TM), 128)
    lane = lax.broadcasted_iota(jnp.int32, (FINE, 128), 1)
    row = lax.broadcasted_iota(jnp.int32, (FINE, 128), 0)
    cross = lane + (FINE - 1) - row >= 128
    for r in range(8):
        for k in range(begin if begin == 0 else begin + 1, end + 1):
            wide = jnp.broadcast_to(rec_ref[r : r + 1, pl.ds(base + k * 128, 128)], (FINE, 128))
            turned = pltpu.roll(wide, 128 - (FINE - 1), 1, stride=1, stride_axis=0)
            if k > 0:
                h_ref[FINE * r : FINE * r + FINE, (k - 1) * 128 : k * 128] = jnp.where(cross, turned, before[r]).astype(bf16)
            before[r] = turned


def multiply(src_ref, h_ref, chunks, prepare_chunk):
    tiles = DEPTH // 128
    summed = None
    for n in range(chunks):
        begin, end = tiles * n // chunks, tiles * (n + 1) // chunks
        prepare_chunk(begin, end)
        term = lax.dot_general(
            src_ref[:, 128 + 128 * begin : 128 + 128 * end],
            h_ref[:, 128 * begin : 128 * end],
            (((1,), (1,)), ((), ())),
            preferred_element_type=f32,
        )
        summed = term if summed is None else summed + term
    return summed


def arrange(summed, emit):
    summed = summed * (1.0 / math.sqrt(TIME))
    lane = lax.broadcasted_iota(jnp.int32, (32, 128), 1)
    spot = [FINE * q + FINE - 1 - lane % FINE for q in range(4)]
    for half in range(2):
        for q in range(4):
            for j in range(2):
                rows = None
                for i in range(4):
                    at = 128 * j + 32 * i
                    moved = jnp.take_along_axis(summed[at : at + 32, 128 * half : 128 * half + 128], spot[q], axis=1)
                    rows = moved if rows is None else jnp.where(lane // FINE == i, moved, rows)
                emit(j, 4 * half + q, rows)


def first_kernel(pieces_ref, h_ref, part_ref, rec_ref, src_ref):
    start_sources(src_ref)
    start_receivers(pieces_ref, rec_ref)
    sources, receivers = [None] * 4, [None] * 8

    def chunk(begin, end):
        load_sources(pieces_ref, src_ref, begin, end, sources)
        spread_receivers(rec_ref, h_ref, begin, end, receivers)

    def emit(j, r, rows):
        part_ref[r, j] = rows

    arrange(multiply(src_ref, h_ref, CHUNKS1, chunk), emit)


def second_kernel(pieces_ref, h_ref, part_ref, out_hbm, src_ref, out_ref, sems):
    start_sources(src_ref)
    sources = [None] * 4

    def chunk(begin, end):
        load_sources(pieces_ref, src_ref, begin, end, sources)

    first = lax.axis_index("core") == 0
    low = lax.broadcasted_iota(jnp.int32, (8, 128), 0) < 4
    moves = []

    def emit(j, r, rows):
        mine = part_ref[r, j]
        for a in range(4):
            x, y = mine[8 * a : 8 * a + 8], rows[8 * a : 8 * a + 8]
            x, y = jnp.where(first, x, y), jnp.where(first, y, x)
            lags = slice(128 * j, 128 * j + 128)
            out_ref[r, 2 * a, :, lags] = jnp.where(low, x, pltpu.roll(y, 4, 0))
            out_ref[r, 2 * a + 1, :, lags] = jnp.where(low, pltpu.roll(x, 4, 0), y)
        if j == 1:
            move = pltpu.make_async_copy(out_ref.at[r], out_hbm.at[:, r], sems.at[r])
            move.start()
            moves.append(move)

    arrange(multiply(src_ref, h_ref, CHUNKS2, chunk), emit)
    for move in moves:
        move.wait()


CHUNKS1, CHUNKS2 = 5, 5
COST = pl.CostEstimate(flops=2 * 256 * 256 * DEPTH, bytes_accessed=4 << 20, transcendentals=0)
LARGE = pltpu.CompilerParams(vmem_limit_bytes=16 << 20)
SOURCES = pltpu.VMEM((256, 128 + DEPTH), bf16)


def on_device(traces, validity, owners):
    blocks, mine, owners = prepare(traces, validity, owners)
    gathered = lax.all_to_all(blocks, NAMES, 0, 0, axis_index_groups=CHAN_GROUPS)
    own = lax.all_to_all(pick(owners, mine, gathered), NAMES, 0, 0, axis_index_groups=TM_GROUPS)
    other = lax.ppermute(own, "core", [(0, 1), (1, 0)])
    spread, part = pl.pallas_call(
        first_kernel,
        out_shape=(jax.ShapeDtypeStruct((256, DEPTH), bf16), jax.ShapeDtypeStruct((8, 2, 32, 128), f32)),
        in_specs=[VMEM],
        out_specs=(VMEM, VMEM),
        scratch_shapes=[pltpu.VMEM((8, LAG + TIME + 1280), f32), SOURCES],
        compiler_params=LARGE,
        cost_estimate=COST,
    )(own)
    return pl.pallas_call(
        second_kernel,
        out_shape=jax.ShapeDtypeStruct((8, 8, 8, 256), f32),
        in_specs=[VMEM] * 3,
        out_specs=pl.BlockSpec(memory_space=pltpu.HBM),
        scratch_shapes=[SOURCES, pltpu.VMEM((8, 8, 8, 256), f32), pltpu.SemaphoreType.DMA((8,))],
        compiler_params=LARGE,
        cost_estimate=COST,
    )(other, spread, part)


def solution(mesh):
    fine = Mesh(mesh.devices.reshape(2, 8, 2, 2, 4), NAMES)
    return jax.shard_map(
        on_device,
        mesh=fine,
        in_specs=(P(CHAN, TM), P(CHAN), P()),
        out_specs=P(None, CHAN, None, TM),
        check_vma=False,
    )
```

```python
import math

import jax
import jax.numpy as jnp
from jax import lax
from jax.experimental import pallas as pl
from jax.experimental.pallas import tpu as pltpu
from jax.sharding import Mesh, PartitionSpec as P

LAG = 1024
TIME = 6144
PIECE = 768
FINE = 32
DEPTH = 6400
NAMES = ("y_lo", "z", "core", "y_hi", "x")
CHAN = ("y_lo", "z", "core")
TM = ("y_hi", "x")
C_STRIDE, C_FIRST, C_STEP = (1, 2, 16), (1, 5, 1), 1
T_STRIDE, T_FIRST, T_STEP = (4, 1), (1, 2), 1


def chan_place(device):
    lo, z, core = device // 16, device // 2 % 8, device % 2
    place = C_STRIDE[0] * ((lo + C_FIRST[0]) % 2) + C_STRIDE[2] * ((core + C_FIRST[2]) % 2)
    return place + C_STRIDE[1] * ((C_STEP * (z + 8 - C_FIRST[1])) % 8)


def tm_place(device):
    hi, x = device // 4, device % 4
    return T_STRIDE[0] * ((hi + T_FIRST[0]) % 2) + T_STRIDE[1] * ((T_STEP * (x + 4 - T_FIRST[1])) % 4)


CHAN_ORDER = sorted(range(32), key=chan_place)
TM_ORDER = sorted(range(8), key=tm_place)
CHAN_GROUPS = [[8 * c + m for c in CHAN_ORDER] for m in range(8)]
TM_GROUPS = [[8 * c + m for m in TM_ORDER] for c in range(32)]
f32, bf16 = jnp.float32, jnp.bfloat16
VMEM = pl.BlockSpec(memory_space=pltpu.VMEM)
SMALL = pltpu.CompilerParams(vmem_limit_bytes=4 << 20)


def prepare_kernel(traces_hbm, validity_hbm, owners_hbm, blocks_ref, mine_ref, owners_ref, traces_ref, validity_ref, sems):
    moves = [
        pltpu.make_async_copy(src, dst, sems.at[n])
        for n, (src, dst) in enumerate(
            ((traces_hbm, traces_ref), (validity_hbm, validity_ref), (owners_hbm, owners_ref))
        )
    ]
    for move in moves:
        move.start()
    for move in moves:
        move.wait()
    row = lax.broadcasted_iota(jnp.int32, (8, 8), 0)
    lane = lax.broadcasted_iota(jnp.int32, (8, 8), 1)
    flags = jnp.broadcast_to(validity_ref[...].astype(f32), (8, 8))
    flags = jnp.sum(jnp.where(row == lane, flags, 0.0), axis=1, keepdims=True)
    usable = (traces_ref[...].astype(f32) * flags).astype(bf16)
    mine_ref[...] = usable
    for place, device in enumerate(CHAN_ORDER):
        half = device % 2
        blocks_ref[place] = usable[4 * half : 4 * half + 4]


def prepare(traces, validity, owners):
    inputs = [pltpu.with_memory_space_constraint(v, pltpu.HBM) for v in (traces, validity.reshape(1, 8), owners.reshape(1, 8))]
    return pl.pallas_call(
        prepare_kernel,
        out_shape=(
            jax.ShapeDtypeStruct((32, 4, PIECE), bf16),
            jax.ShapeDtypeStruct((8, PIECE), bf16),
            jax.ShapeDtypeStruct((1, 8), jnp.int32),
        ),
        in_specs=[pl.BlockSpec(memory_space=pltpu.HBM)] * 3,
        out_specs=(VMEM, VMEM, VMEM),
        scratch_shapes=[pltpu.VMEM((8, PIECE), bf16), pltpu.VMEM((1, 8), jnp.int32), pltpu.SemaphoreType.DMA((3,))],
        compiler_params=SMALL,
    )(*inputs)


def pick_kernel(owners_ref, mine_ref, gathered_ref, out_ref):
    lane = lax.broadcasted_iota(jnp.int32, (1, 8), 1)
    owners = owners_ref[...]
    for peer in range(8):
        out_ref[peer, :8, :] = mine_ref[...]
    for s in range(8):
        block = gathered_ref[chan_place(jnp.sum(jnp.where(lane == s, owners, 0)))]
        for peer in range(8):
            out_ref[peer, 8 + 4 * s : 12 + 4 * s, :] = block


def pick(owners, mine, gathered):
    return pl.pallas_call(
        pick_kernel,
        out_shape=jax.ShapeDtypeStruct((8, 40, PIECE), bf16),
        in_specs=[VMEM] * 3,
        out_specs=VMEM,
        compiler_params=SMALL,
    )(owners, mine, gathered)


def start_sources(src_ref):
    src_ref[:, :128] = jnp.zeros((128, 128), bf16)


def load_sources(pieces_ref, src_ref, begin, end, before):
    lane = lax.broadcasted_iota(jnp.int32, (32, 128), 1)
    for k in range(begin, end):
        t = 128 * k
        if t < TIME:
            tile = pieces_ref[tm_place(t // PIECE), 8:40, t % PIECE : t % PIECE + 128]
        else:
            tile = jnp.zeros((32, 128), bf16)
        wide = tile.astype(f32)
        for i in range(4):
            if i == 0:
                value = tile
            else:
                turned = pltpu.roll(wide, FINE * i, 1)
                last = before[i] if before[i] is not None else jnp.zeros((32, 128), f32)
                value = jnp.where(lane < FINE * i, last, turned).astype(bf16)
                before[i] = turned
            src_ref[32 * i : 32 * i + 32, 128 * k + 128 : 128 * k + 256] = value


def start_receivers(pieces_ref, rec_ref):
    rec_ref[:, :LAG] = jnp.zeros((8, LAG), f32)
    rec_ref[:, LAG + TIME :] = jnp.zeros((8, rec_ref.shape[1] - LAG - TIME), f32)
    for piece in range(8):
        at = LAG + PIECE * piece
        rec_ref[:, at : at + PIECE] = pieces_ref[tm_place(piece), :8, :].astype(f32)


def spread_receivers(rec_ref, h_ref, begin, end, before):
    base = pl.multiple_of(256 * lax.axis_index(TM), 128)
    lane = lax.broadcasted_iota(jnp.int32, (FINE, 128), 1)
    row = lax.broadcasted_iota(jnp.int32, (FINE, 128), 0)
    cross = lane + (FINE - 1) - row >= 128
    for r in range(8):
        for k in range(begin if begin == 0 else begin + 1, end + 1):
            wide = jnp.broadcast_to(rec_ref[r : r + 1, pl.ds(base + k * 128, 128)], (FINE, 128))
            turned = pltpu.roll(wide, 128 - (FINE - 1), 1, stride=1, stride_axis=0)
            if k > 0:
                h_ref[FINE * r : FINE * r + FINE, (k - 1) * 128 : k * 128] = jnp.where(cross, turned, before[r]).astype(bf16)
            before[r] = turned


def multiply(src_ref, h_ref, chunks, prepare_chunk):
    tiles = DEPTH // 128
    summed = None
    for n in range(chunks):
        begin, end = tiles * n // chunks, tiles * (n + 1) // chunks
        prepare_chunk(begin, end)
        shifted = [src_ref[:, 128 * (begin + 1 - j) : 128 * (end + 1 - j)] for j in range(2)]
        term = lax.dot_general(
            jnp.concatenate(shifted, axis=0),
            h_ref[:, 128 * begin : 128 * end],
            (((1,), (1,)), ((), ())),
            preferred_element_type=f32,
        )
        summed = term if summed is None else summed + term
    return summed


def arrange(summed, emit):
    summed = summed * (1.0 / math.sqrt(TIME))
    lane = lax.broadcasted_iota(jnp.int32, (32, 128), 1)
    group = lane // FINE
    spot = [(group + q) % 4 * FINE + FINE - 1 - lane % FINE for q in range(4)]
    for half in range(2):
        turned = [[summed[128 * j + 32 * i : 128 * j + 32 * i + 32, 128 * half : 128 * half + 128] for i in range(4)] for j in range(2)]
        turned = [[t[0]] + [pltpu.roll(t[i], FINE * i, 1) for i in range(1, 4)] for t in turned]
        for q in range(4):
            for j in range(2):
                rows = turned[j][0]
                for i in range(1, 4):
                    rows = jnp.where(group == (q + i) % 4, turned[j][i], rows)
                emit(j, 4 * half + q, jnp.take_along_axis(rows, spot[q], axis=1))


def first_kernel(pieces_ref, h_ref, part_ref, rec_ref, src_ref):
    start_sources(src_ref)
    start_receivers(pieces_ref, rec_ref)
    sources, receivers = [None] * 4, [None] * 8

    def chunk(begin, end):
        load_sources(pieces_ref, src_ref, begin, end, sources)
        spread_receivers(rec_ref, h_ref, begin, end, receivers)

    def emit(j, r, rows):
        part_ref[r, j] = rows

    arrange(multiply(src_ref, h_ref, CHUNKS1, chunk), emit)


def second_kernel(pieces_ref, h_ref, part_ref, out_hbm, src_ref, out_ref, sems):
    start_sources(src_ref)
    sources = [None] * 4

    def chunk(begin, end):
        load_sources(pieces_ref, src_ref, begin, end, sources)

    first = lax.axis_index("core") == 0
    low = lax.broadcasted_iota(jnp.int32, (8, 128), 0) < 4
    moves = []

    def emit(j, r, rows):
        mine = part_ref[r, j]
        for a in range(4):
            x, y = mine[8 * a : 8 * a + 8], rows[8 * a : 8 * a + 8]
            x, y = jnp.where(first, x, y), jnp.where(first, y, x)
            lags = slice(128 * j, 128 * j + 128)
            out_ref[r, 2 * a, :, lags] = jnp.where(low, x, pltpu.roll(y, 4, 0))
            out_ref[r, 2 * a + 1, :, lags] = jnp.where(low, pltpu.roll(x, 4, 0), y)
        if j == 1:
            move = pltpu.make_async_copy(out_ref.at[r], out_hbm.at[:, r], sems.at[r])
            move.start()
            moves.append(move)

    arrange(multiply(src_ref, h_ref, CHUNKS2, chunk), emit)
    for move in moves:
        move.wait()


CHUNKS1, CHUNKS2 = 5, 5
COST = pl.CostEstimate(flops=2 * 256 * 256 * DEPTH, bytes_accessed=4 << 20, transcendentals=0)
LARGE = pltpu.CompilerParams(vmem_limit_bytes=16 << 20)
SOURCES = pltpu.VMEM((128, 128 + DEPTH), bf16)


def on_device(traces, validity, owners):
    blocks, mine, owners = prepare(traces, validity, owners)
    gathered = lax.all_to_all(blocks, NAMES, 0, 0, axis_index_groups=CHAN_GROUPS)
    own = lax.all_to_all(pick(owners, mine, gathered), NAMES, 0, 0, axis_index_groups=TM_GROUPS)
    other = lax.ppermute(own, "core", [(0, 1), (1, 0)])
    spread, part = pl.pallas_call(
        first_kernel,
        out_shape=(jax.ShapeDtypeStruct((256, DEPTH), bf16), jax.ShapeDtypeStruct((8, 2, 32, 128), f32)),
        in_specs=[VMEM],
        out_specs=(VMEM, VMEM),
        scratch_shapes=[pltpu.VMEM((8, LAG + TIME + 1280), f32), SOURCES],
        compiler_params=LARGE,
        cost_estimate=COST,
    )(own)
    return pl.pallas_call(
        second_kernel,
        out_shape=jax.ShapeDtypeStruct((8, 8, 8, 256), f32),
        in_specs=[VMEM] * 3,
        out_specs=pl.BlockSpec(memory_space=pltpu.HBM),
        scratch_shapes=[SOURCES, pltpu.VMEM((8, 8, 8, 256), f32), pltpu.SemaphoreType.DMA((8,))],
        compiler_params=LARGE,
        cost_estimate=COST,
    )(other, spread, part)


def solution(mesh):
    fine = Mesh(mesh.devices.reshape(2, 8, 2, 2, 4), NAMES)
    return jax.shard_map(
        on_device,
        mesh=fine,
        in_specs=(P(CHAN, TM), P(CHAN), P()),
        out_specs=P(None, CHAN, None, TM),
        check_vma=False,
    )
```

```python
import math

import jax
import jax.numpy as jnp
from jax import lax
from jax.experimental import pallas as pl
from jax.experimental.pallas import tpu as pltpu
from jax.sharding import Mesh, PartitionSpec as P

LAG = 1024
TIME = 6144
PIECE = 768
FINE = 32
DEPTH = 6400
NAMES = ("y_lo", "z", "core", "y_hi", "x")
CHAN = ("y_lo", "z", "core")
TM = ("y_hi", "x")
C_STRIDE, C_FIRST, C_STEP = (1, 2, 16), (1, 5, 1), 1
T_STRIDE, T_FIRST, T_STEP = ((4, 1), (1, 2)), ((1, 2), (1, 2)), (1, 1)


def chan_place(device):
    lo, z, core = device // 16, device // 2 % 8, device % 2
    place = C_STRIDE[0] * ((lo + C_FIRST[0]) % 2) + C_STRIDE[2] * ((core + C_FIRST[2]) % 2)
    return place + C_STRIDE[1] * ((C_STEP * (z + 8 - C_FIRST[1])) % 8)


def tm_place(device, core):
    hi, x = device // 4, device % 4
    place = T_STRIDE[core][0] * ((hi + T_FIRST[core][0]) % 2)
    return place + T_STRIDE[core][1] * ((T_STEP[core] * (x + 4 - T_FIRST[core][1])) % 4)


def tm_places(core):
    return [jnp.where(core == 0, tm_place(m, 0), tm_place(m, 1)) for m in range(8)]


CHAN_ORDER = sorted(range(32), key=chan_place)
TM_ORDER = [sorted(range(8), key=lambda m: tm_place(m, core)) for core in range(2)]
CHAN_GROUPS = [[8 * c + m for c in CHAN_ORDER] for m in range(8)]
TM_GROUPS = [[8 * c + m for m in TM_ORDER[c % 2]] for c in range(32)]
f32, bf16 = jnp.float32, jnp.bfloat16
VMEM = pl.BlockSpec(memory_space=pltpu.VMEM)
SMALL = pltpu.CompilerParams(vmem_limit_bytes=4 << 20)


def prepare_kernel(traces_hbm, validity_hbm, owners_hbm, blocks_ref, mine_ref, owners_ref, traces_ref, validity_ref, sems):
    moves = [
        pltpu.make_async_copy(src, dst, sems.at[n])
        for n, (src, dst) in enumerate(
            ((traces_hbm, traces_ref), (validity_hbm, validity_ref), (owners_hbm, owners_ref))
        )
    ]
    for move in moves:
        move.start()
    for move in moves:
        move.wait()
    row = lax.broadcasted_iota(jnp.int32, (8, 8), 0)
    lane = lax.broadcasted_iota(jnp.int32, (8, 8), 1)
    flags = jnp.broadcast_to(validity_ref[...].astype(f32), (8, 8))
    flags = jnp.sum(jnp.where(row == lane, flags, 0.0), axis=1, keepdims=True)
    usable = (traces_ref[...].astype(f32) * flags).astype(bf16)
    mine_ref[...] = usable
    for place, device in enumerate(CHAN_ORDER):
        half = device % 2
        blocks_ref[place] = usable[4 * half : 4 * half + 4]


def prepare(traces, validity, owners):
    inputs = [pltpu.with_memory_space_constraint(v, pltpu.HBM) for v in (traces, validity.reshape(1, 8), owners.reshape(1, 8))]
    return pl.pallas_call(
        prepare_kernel,
        out_shape=(
            jax.ShapeDtypeStruct((32, 4, PIECE), bf16),
            jax.ShapeDtypeStruct((8, PIECE), bf16),
            jax.ShapeDtypeStruct((1, 8), jnp.int32),
        ),
        in_specs=[pl.BlockSpec(memory_space=pltpu.HBM)] * 3,
        out_specs=(VMEM, VMEM, VMEM),
        scratch_shapes=[pltpu.VMEM((8, PIECE), bf16), pltpu.VMEM((1, 8), jnp.int32), pltpu.SemaphoreType.DMA((3,))],
        compiler_params=SMALL,
    )(*inputs)


def pick_kernel(owners_ref, mine_ref, gathered_ref, out_ref):
    lane = lax.broadcasted_iota(jnp.int32, (1, 8), 1)
    places = chan_place(owners_ref[...])
    for peer in range(8):
        out_ref[peer, :8, :] = mine_ref[...]
    for s in range(8):
        block = gathered_ref[jnp.sum(jnp.where(lane == s, places, 0))]
        for peer in range(8):
            out_ref[peer, 8 + 4 * s : 12 + 4 * s, :] = block


def pick(owners, mine, gathered):
    return pl.pallas_call(
        pick_kernel,
        out_shape=jax.ShapeDtypeStruct((8, 40, PIECE), bf16),
        in_specs=[VMEM] * 3,
        out_specs=VMEM,
        compiler_params=SMALL,
    )(owners, mine, gathered)


def start_sources(src_ref):
    src_ref[:, :128] = jnp.zeros((128, 128), bf16)


def load_sources(pieces_ref, places, src_ref, begin, end, before):
    lane = lax.broadcasted_iota(jnp.int32, (32, 128), 1)
    for k in range(begin, end):
        t = 128 * k
        if t < TIME:
            tile = pieces_ref[places[t // PIECE], 8:40, t % PIECE : t % PIECE + 128]
        else:
            tile = jnp.zeros((32, 128), bf16)
        wide = tile.astype(f32)
        for i in range(4):
            if i == 0:
                value = tile
            else:
                turned = pltpu.roll(wide, FINE * i, 1)
                last = before[i] if before[i] is not None else jnp.zeros((32, 128), f32)
                value = jnp.where(lane < FINE * i, last, turned).astype(bf16)
                before[i] = turned
            src_ref[32 * i : 32 * i + 32, 128 * k + 128 : 128 * k + 256] = value


def start_receivers(pieces_ref, places, rec_ref):
    rec_ref[:, :LAG] = jnp.zeros((8, LAG), f32)
    rec_ref[:, LAG + TIME :] = jnp.zeros((8, rec_ref.shape[1] - LAG - TIME), f32)
    for piece in range(8):
        at = LAG + PIECE * piece
        rec_ref[:, at : at + PIECE] = pieces_ref[places[piece], :8, :].astype(f32)


def spread_receivers(rec_ref, h_ref, begin, end, before):
    base = pl.multiple_of(256 * lax.axis_index(TM), 128)
    lane = lax.broadcasted_iota(jnp.int32, (FINE, 128), 1)
    row = lax.broadcasted_iota(jnp.int32, (FINE, 128), 0)
    cross = lane + (FINE - 1) - row >= 128
    for r in range(8):
        for k in range(begin if begin == 0 else begin + 1, end + 1):
            wide = jnp.broadcast_to(rec_ref[r : r + 1, pl.ds(base + k * 128, 128)], (FINE, 128))
            turned = pltpu.roll(wide, 128 - (FINE - 1), 1, stride=1, stride_axis=0).astype(bf16)
            if k > 0:
                h_ref[FINE * r : FINE * r + FINE, (k - 1) * 128 : k * 128] = jnp.where(cross, turned, before[r])
            before[r] = turned


def multiply(src_ref, h_ref, chunks, prepare_chunk):
    tiles = DEPTH // 128
    summed = None
    for n in range(chunks):
        begin, end = tiles * n // chunks, tiles * (n + 1) // chunks
        prepare_chunk(begin, end)
        shifted = [src_ref[:, 128 * (begin + 1 - j) : 128 * (end + 1 - j)] for j in range(2)]
        term = lax.dot_general(
            jnp.concatenate(shifted, axis=0),
            h_ref[:, 128 * begin : 128 * end],
            (((1,), (1,)), ((), ())),
            preferred_element_type=f32,
        )
        summed = term if summed is None else summed + term
    return summed


def arrange(summed, emit):
    summed = summed * (1.0 / math.sqrt(TIME))
    lane = lax.broadcasted_iota(jnp.int32, (32, 128), 1)
    group = lane // FINE
    spot = [(group + q) % 4 * FINE + FINE - 1 - lane % FINE for q in range(4)]
    for half in range(2):
        turned = [[summed[128 * j + 32 * i : 128 * j + 32 * i + 32, 128 * half : 128 * half + 128] for i in range(4)] for j in range(2)]
        turned = [[t[0]] + [pltpu.roll(t[i], FINE * i, 1) for i in range(1, 4)] for t in turned]
        for q in range(4):
            for j in range(2):
                rows = turned[j][0]
                for i in range(1, 4):
                    rows = jnp.where(group == (q + i) % 4, turned[j][i], rows)
                emit(j, 4 * half + q, jnp.take_along_axis(rows, spot[q], axis=1))


def first_kernel(pieces_ref, h_ref, part_ref, rec_ref, src_ref):
    places = tm_places(lax.axis_index("core"))
    start_sources(src_ref)
    start_receivers(pieces_ref, places, rec_ref)
    sources, receivers = [None] * 4, [None] * 8

    def chunk(begin, end):
        load_sources(pieces_ref, places, src_ref, begin, end, sources)
        spread_receivers(rec_ref, h_ref, begin, end, receivers)

    def emit(j, r, rows):
        part_ref[r, j] = rows

    arrange(multiply(src_ref, h_ref, CHUNKS1, chunk), emit)


def second_kernel(pieces_ref, h_ref, part_ref, out_hbm, src_ref, out_ref, sems):
    places = tm_places(1 - lax.axis_index("core"))
    start_sources(src_ref)
    sources = [None] * 4

    def chunk(begin, end):
        load_sources(pieces_ref, places, src_ref, begin, end, sources)

    first = lax.axis_index("core") == 0
    low = lax.broadcasted_iota(jnp.int32, (8, 128), 0) < 4
    moves = []

    def emit(j, r, rows):
        mine = part_ref[r, j]
        for a in range(4):
            x, y = mine[8 * a : 8 * a + 8], rows[8 * a : 8 * a + 8]
            x, y = jnp.where(first, x, y), jnp.where(first, y, x)
            lags = slice(128 * j, 128 * j + 128)
            out_ref[r, 2 * a, :, lags] = jnp.where(low, x, pltpu.roll(y, 4, 0))
            out_ref[r, 2 * a + 1, :, lags] = jnp.where(low, pltpu.roll(x, 4, 0), y)
        if j == 1:
            move = pltpu.make_async_copy(out_ref.at[r], out_hbm.at[:, r], sems.at[r])
            move.start()
            moves.append(move)

    arrange(multiply(src_ref, h_ref, CHUNKS2, chunk), emit)
    for move in moves:
        move.wait()


CHUNKS1, CHUNKS2 = 5, 5
COST = pl.CostEstimate(flops=2 * 256 * 256 * DEPTH, bytes_accessed=4 << 20, transcendentals=0)
LARGE = pltpu.CompilerParams(vmem_limit_bytes=16 << 20)
SOURCES = pltpu.VMEM((128, 128 + DEPTH), bf16)


def on_device(traces, validity, owners):
    blocks, mine, owners = prepare(traces, validity, owners)
    gathered = lax.all_to_all(blocks, NAMES, 0, 0, axis_index_groups=CHAN_GROUPS)
    own = lax.all_to_all(pick(owners, mine, gathered), NAMES, 0, 0, axis_index_groups=TM_GROUPS)
    other = lax.ppermute(own, "core", [(0, 1), (1, 0)])
    spread, part = pl.pallas_call(
        first_kernel,
        out_shape=(jax.ShapeDtypeStruct((256, DEPTH), bf16), jax.ShapeDtypeStruct((8, 2, 32, 128), f32)),
        in_specs=[VMEM],
        out_specs=(VMEM, VMEM),
        scratch_shapes=[pltpu.VMEM((8, LAG + TIME + 1280), f32), SOURCES],
        compiler_params=LARGE,
        cost_estimate=COST,
    )(own)
    return pl.pallas_call(
        second_kernel,
        out_shape=jax.ShapeDtypeStruct((8, 8, 8, 256), f32),
        in_specs=[VMEM] * 3,
        out_specs=pl.BlockSpec(memory_space=pltpu.HBM),
        scratch_shapes=[SOURCES, pltpu.VMEM((8, 8, 8, 256), f32), pltpu.SemaphoreType.DMA((8,))],
        compiler_params=LARGE,
        cost_estimate=COST,
    )(other, spread, part)


def solution(mesh):
    fine = Mesh(mesh.devices.reshape(2, 8, 2, 2, 4), NAMES)
    return jax.shard_map(
        on_device,
        mesh=fine,
        in_specs=(P(CHAN, TM), P(CHAN), P()),
        out_specs=P(None, CHAN, None, TM),
        check_vma=False,
    )
```

```python
import math

import jax
import jax.numpy as jnp
from jax import lax
from jax.experimental import pallas as pl
from jax.experimental.pallas import tpu as pltpu
from jax.sharding import Mesh, PartitionSpec as P

LAG = 1024
TIME = 6144
PIECE = 768
FINE = 32
DEPTH = 6400
NAMES = ("y_lo", "z", "core", "y_hi", "x")
CHAN = ("y_lo", "z", "core")
TM = ("y_hi", "x")
C_STRIDE, C_FIRST, C_STEP = (1, 2, 16), (1, 5, 1), 1
T_STRIDE, T_FIRST, T_STEP = ((4, 1), (1, 2)), ((1, 2), (1, 2)), (1, 1)


def chan_place(device):
    lo, z, core = device // 16, device // 2 % 8, device % 2
    place = C_STRIDE[0] * ((lo + C_FIRST[0]) % 2) + C_STRIDE[2] * ((core + C_FIRST[2]) % 2)
    return place + C_STRIDE[1] * ((C_STEP * (z + 8 - C_FIRST[1])) % 8)


def tm_place(device, core):
    hi, x = device // 4, device % 4
    place = T_STRIDE[core][0] * ((hi + T_FIRST[core][0]) % 2)
    return place + T_STRIDE[core][1] * ((T_STEP[core] * (x + 4 - T_FIRST[core][1])) % 4)


def tm_places(core):
    return [jnp.where(core == 0, tm_place(m, 0), tm_place(m, 1)) for m in range(8)]


CHAN_ORDER = sorted(range(32), key=chan_place)
TM_ORDER = [sorted(range(8), key=lambda m: tm_place(m, core)) for core in range(2)]
CHAN_GROUPS = [[8 * c + m for c in CHAN_ORDER] for m in range(8)]
TM_GROUPS = [[8 * c + m for m in TM_ORDER[c % 2]] for c in range(32)]
f32, bf16 = jnp.float32, jnp.bfloat16
VMEM = pl.BlockSpec(memory_space=pltpu.VMEM)
SMALL = pltpu.CompilerParams(vmem_limit_bytes=4 << 20)


def prepare_kernel(traces_hbm, validity_hbm, owners_hbm, blocks_ref, mine_ref, owners_ref, traces_ref, validity_ref, sems):
    moves = [
        pltpu.make_async_copy(src, dst, sems.at[n])
        for n, (src, dst) in enumerate(
            ((traces_hbm, traces_ref), (validity_hbm, validity_ref), (owners_hbm, owners_ref))
        )
    ]
    for move in moves:
        move.start()
    for move in moves:
        move.wait()
    row = lax.broadcasted_iota(jnp.int32, (8, 8), 0)
    lane = lax.broadcasted_iota(jnp.int32, (8, 8), 1)
    flags = jnp.broadcast_to(validity_ref[...].astype(f32), (8, 8))
    flags = jnp.sum(jnp.where(row == lane, flags, 0.0), axis=1, keepdims=True)
    usable = (traces_ref[...].astype(f32) * flags).astype(bf16)
    mine_ref[...] = usable
    for place, device in enumerate(CHAN_ORDER):
        half = device % 2
        blocks_ref[place] = usable[4 * half : 4 * half + 4]


def prepare(traces, validity, owners):
    inputs = [pltpu.with_memory_space_constraint(v, pltpu.HBM) for v in (traces, validity.reshape(1, 8), owners.reshape(1, 8))]
    return pl.pallas_call(
        prepare_kernel,
        out_shape=(
            jax.ShapeDtypeStruct((32, 4, PIECE), bf16),
            jax.ShapeDtypeStruct((8, PIECE), bf16),
            jax.ShapeDtypeStruct((1, 8), jnp.int32),
        ),
        in_specs=[pl.BlockSpec(memory_space=pltpu.HBM)] * 3,
        out_specs=(VMEM, VMEM, VMEM),
        scratch_shapes=[pltpu.VMEM((8, PIECE), bf16), pltpu.VMEM((1, 8), jnp.int32), pltpu.SemaphoreType.DMA((3,))],
        compiler_params=SMALL,
    )(*inputs)


def pick_kernel(owners_ref, mine_ref, gathered_ref, out_ref):
    lane = lax.broadcasted_iota(jnp.int32, (1, 8), 1)
    places = chan_place(owners_ref[...])
    for peer in range(8):
        out_ref[peer, :8, :] = mine_ref[...]
    for s in range(8):
        block = gathered_ref[jnp.sum(jnp.where(lane == s, places, 0))]
        for peer in range(8):
            out_ref[peer, 8 + 4 * s : 12 + 4 * s, :] = block


def pick(owners, mine, gathered):
    return pl.pallas_call(
        pick_kernel,
        out_shape=jax.ShapeDtypeStruct((8, 40, PIECE), bf16),
        in_specs=[VMEM] * 3,
        out_specs=VMEM,
        compiler_params=SMALL,
    )(owners, mine, gathered)


def start_sources(src_ref):
    src_ref[:, :128] = jnp.zeros((128, 128), bf16)


def load_sources(pieces_ref, places, src_ref, begin, end, before):
    lane = lax.broadcasted_iota(jnp.int32, (32, 128), 1)
    for k in range(begin, end):
        t = 128 * k
        if t < TIME:
            tile = pieces_ref[places[t // PIECE], 8:40, t % PIECE : t % PIECE + 128]
        else:
            tile = jnp.zeros((32, 128), bf16)
        wide = tile.astype(f32)
        for i in range(4):
            if i == 0:
                value = tile
            else:
                turned = pltpu.roll(wide, FINE * i, 1)
                last = before[i] if before[i] is not None else jnp.zeros((32, 128), f32)
                value = jnp.where(lane < FINE * i, last, turned).astype(bf16)
                before[i] = turned
            src_ref[32 * i : 32 * i + 32, 128 * k + 128 : 128 * k + 256] = value


def start_receivers(pieces_ref, places, rec_ref):
    rec_ref[:, :LAG] = jnp.zeros((8, LAG), f32)
    rec_ref[:, LAG + TIME :] = jnp.zeros((8, rec_ref.shape[1] - LAG - TIME), f32)
    for piece in range(8):
        at = LAG + PIECE * piece
        rec_ref[:, at : at + PIECE] = pieces_ref[places[piece], :8, :].astype(f32)


def spread_receivers(rec_ref, h_ref, begin, end, before):
    base = pl.multiple_of(256 * lax.axis_index(TM), 128)
    lane = lax.broadcasted_iota(jnp.int32, (FINE, 128), 1)
    row = lax.broadcasted_iota(jnp.int32, (FINE, 128), 0)
    cross = lane + (FINE - 1) - row >= 128
    for r in range(8):
        for k in range(begin if begin == 0 else begin + 1, end + 1):
            wide = jnp.broadcast_to(rec_ref[r : r + 1, pl.ds(base + k * 128, 128)], (FINE, 128))
            turned = pltpu.roll(wide, 128 - (FINE - 1), 1, stride=1, stride_axis=0).astype(bf16)
            if k > 0:
                h_ref[FINE * r : FINE * r + FINE, (k - 1) * 128 : k * 128] = jnp.where(cross, turned, before[r])
            before[r] = turned


def multiply(src_ref, h_ref, chunks, prepare_chunk):
    summed = None
    for n in range(len(chunks) - 1):
        begin, end = chunks[n], chunks[n + 1]
        prepare_chunk(begin, end)
        shifted = [src_ref[:, 128 * (begin + 1 - j) : 128 * (end + 1 - j)] for j in range(2)]
        term = lax.dot_general(
            jnp.concatenate(shifted, axis=0),
            h_ref[:, 128 * begin : 128 * end],
            (((1,), (1,)), ((), ())),
            preferred_element_type=f32,
        )
        summed = term if summed is None else summed + term
    return summed


def arrange(summed, emit):
    summed = summed * (1.0 / math.sqrt(TIME))
    lane = lax.broadcasted_iota(jnp.int32, (32, 128), 1)
    group = lane // FINE
    spot = [(group + q) % 4 * FINE + FINE - 1 - lane % FINE for q in range(4)]
    for half in range(2):
        turned = [[summed[128 * j + 32 * i : 128 * j + 32 * i + 32, 128 * half : 128 * half + 128] for i in range(4)] for j in range(2)]
        turned = [[t[0]] + [pltpu.roll(t[i], FINE * i, 1) for i in range(1, 4)] for t in turned]
        for q in range(4):
            for j in range(2):
                rows = turned[j][0]
                for i in range(1, 4):
                    rows = jnp.where(group == (q + i) % 4, turned[j][i], rows)
                emit(j, 4 * half + q, jnp.take_along_axis(rows, spot[q], axis=1))


def first_kernel(pieces_ref, h_ref, part_ref, rec_ref, src_ref):
    places = tm_places(lax.axis_index("core"))
    start_sources(src_ref)
    start_receivers(pieces_ref, places, rec_ref)
    sources, receivers = [None] * 4, [None] * 8

    def chunk(begin, end):
        load_sources(pieces_ref, places, src_ref, begin, end, sources)
        spread_receivers(rec_ref, h_ref, begin, end, receivers)

    def emit(j, r, rows):
        part_ref[r, j] = rows

    arrange(multiply(src_ref, h_ref, CHUNKS1, chunk), emit)


def second_kernel(pieces_ref, h_ref, part_ref, out_hbm, src_ref, out_ref, sems):
    places = tm_places(1 - lax.axis_index("core"))
    start_sources(src_ref)
    sources = [None] * 4

    def chunk(begin, end):
        load_sources(pieces_ref, places, src_ref, begin, end, sources)

    first = lax.axis_index("core") == 0
    low = lax.broadcasted_iota(jnp.int32, (8, 128), 0) < 4
    moves = []

    def emit(j, r, rows):
        mine = part_ref[r, j]
        for a in range(4):
            x, y = mine[8 * a : 8 * a + 8], rows[8 * a : 8 * a + 8]
            x, y = jnp.where(first, x, y), jnp.where(first, y, x)
            lags = slice(128 * j, 128 * j + 128)
            out_ref[r, 2 * a, :, lags] = jnp.where(low, x, pltpu.roll(y, 4, 0))
            out_ref[r, 2 * a + 1, :, lags] = jnp.where(low, pltpu.roll(x, 4, 0), y)
        if j == 1:
            move = pltpu.make_async_copy(out_ref.at[r], out_hbm.at[:, r], sems.at[r])
            move.start()
            moves.append(move)

    arrange(multiply(src_ref, h_ref, CHUNKS2, chunk), emit)
    for move in moves:
        move.wait()


CHUNKS1, CHUNKS2 = (0, 4, 14, 24, 34, 44, 50), (0, 2, 6, 50)
COST = pl.CostEstimate(flops=2 * 256 * 256 * DEPTH, bytes_accessed=4 << 20, transcendentals=0)
LARGE = pltpu.CompilerParams(vmem_limit_bytes=16 << 20)
SOURCES = pltpu.VMEM((128, 128 + DEPTH), bf16)


def on_device(traces, validity, owners):
    blocks, mine, owners = prepare(traces, validity, owners)
    gathered = lax.all_to_all(blocks, NAMES, 0, 0, axis_index_groups=CHAN_GROUPS)
    own = lax.all_to_all(pick(owners, mine, gathered), NAMES, 0, 0, axis_index_groups=TM_GROUPS)
    other = lax.ppermute(own, "core", [(0, 1), (1, 0)])
    spread, part = pl.pallas_call(
        first_kernel,
        out_shape=(jax.ShapeDtypeStruct((256, DEPTH), bf16), jax.ShapeDtypeStruct((8, 2, 32, 128), f32)),
        in_specs=[VMEM],
        out_specs=(VMEM, VMEM),
        scratch_shapes=[pltpu.VMEM((8, LAG + TIME + 1280), f32), SOURCES],
        compiler_params=LARGE,
        cost_estimate=COST,
    )(own)
    return pl.pallas_call(
        second_kernel,
        out_shape=jax.ShapeDtypeStruct((8, 8, 8, 256), f32),
        in_specs=[VMEM] * 3,
        out_specs=pl.BlockSpec(memory_space=pltpu.HBM),
        scratch_shapes=[SOURCES, pltpu.VMEM((8, 8, 8, 256), f32), pltpu.SemaphoreType.DMA((8,))],
        compiler_params=LARGE,
        cost_estimate=COST,
    )(other, spread, part)


def solution(mesh):
    fine = Mesh(mesh.devices.reshape(2, 8, 2, 2, 4), NAMES)
    return jax.shard_map(
        on_device,
        mesh=fine,
        in_specs=(P(CHAN, TM), P(CHAN), P()),
        out_specs=P(None, CHAN, None, TM),
        check_vma=False,
    )
```
